128 devices in a mesh: lat: 8 (over x, y_hi), lon: 16 (over z, y_lo, core).
Axes of the slice: x: 4, y: 4 (y_hi: 2, y_lo: 2; y = y_hi * 2 + y_lo), z: 4, core: 2. Of those that a mesh axis runs over, the one named last changes fastest.
Arguments:
- features: bfloat16 [256, 384, 2048], P('lat', 'lon'), may hold values from -6 to 6
- atrous_weight: bfloat16 [3, 3, 2048, 256], replicated, may hold values from -0.046875 to 0.046875
- norm_gain: float32 [256], replicated, may hold values from 0.1 to 1.9
- norm_bias: float32 [256], replicated, may hold values from -0.5 to 0.5
- head_weight: float32 [3, 256], replicated, may hold values from -1.5 to 1.5
- labels: int32 [256, 384], P('lat', 'lon'), may hold values from 0 to 2
Outputs:
- mean_loss: float32 [], replicated
- grad_features: bfloat16 [256, 384, 2048], P('lat', 'lon')
- grad_weight: float32 [2048, 3, 3, 256], P('lat', None, None, 'lon')
- grad_gain: float32 [256], replicated
- grad_bias: float32 [256], replicated
- grad_head: float32 [3, 256], replicated
The draws below stay inside these ranges and needn't reach their ends.
All inputs are finite; a program needn't handle non-finite values.
Results may differ from the reference program's by a relative error of at most 0.022.
Values may be sent and summed in bfloat16 or wider, within the bound.
No kernel may reach another device: no remote copies, remote signals or barrier semaphores. Data moves between devices by JAX's collectives and lax.ppermute only.
A program may use at most 192 MiB of HBM per device.

```python
import jax
import jax.numpy as jnp
from jax import lax

CIN = 2048
COUT = 256
CLASSES = 3
RATE = 12
H = 256
W = 384


def touch_ends(entries, key, smallest, high):
    extent = entries.shape
    spot = [jax.random.randint(jax.random.fold_in(key, axis), (), 0, extent[axis]) for axis in range(len(extent))]
    entries = entries.at[tuple(spot)].set(smallest)
    longest = extent.index(max(extent))
    spot[longest] = (spot[longest] + 1) % extent[longest]
    return entries.at[tuple(spot)].set(high)


def block_levels(rng, extent, cuts, least, high):
    level = 1.0
    for dim, parts in cuts:
        steps = jax.random.uniform(jax.random.fold_in(jax.random.fold_in(rng, 6), dim), (parts,), jnp.float32, least / len(cuts), high / len(cuts))
        level = level * jnp.repeat(jnp.exp(steps), extent[dim] // parts).reshape((-1,) + (1,) * (len(extent) - 1 - dim))
    return level


def bell_draw(own_key, extent, scale, bound, shards=(), kind=jnp.bfloat16):
    gain = block_levels(own_key, extent, shards, -0.22, 0.18) if shards else 1.0
    entries = jax.random.normal(own_key, extent, jnp.float32) * scale * gain
    return jnp.minimum(jnp.maximum(entries, -bound), bound).astype(kind)


def setup_inputs(seed: int = 0) -> dict:
    arg_keys = jax.random.split(jax.random.key(seed), 7)
    return {
        "features": bell_draw(arg_keys[0], (H, W, CIN), 1.0, 6.0, ((0, 8), (1, 16))),
        "atrous_weight": bell_draw(arg_keys[1], (3, 3, CIN, COUT), (9 * CIN) ** -0.5, 0.046875),
        "norm_gain": jnp.clip(1.0 + 0.18 * jax.random.normal(arg_keys[2], (COUT,), jnp.float32), 0.1, 1.9),
        "norm_bias": jnp.clip(jax.random.uniform(arg_keys[3], (COUT,), jnp.float32, -0.5, 0.5), -0.5, 0.5),
        "head_weight": bell_draw(arg_keys[4], (CLASSES, COUT), 0.25, 1.5, (), jnp.float32),
        "labels": touch_ends(jax.random.randint(arg_keys[5], (H, W), 0, CLASSES), jax.random.fold_in(arg_keys[5], 1), 0, CLASSES - 1).astype(jnp.int32),
    }


epsilon = 1e-05

def cycle_pad(field):
    lon_padded = jnp.concatenate([field[:, W - RATE:], field, field[:, :RATE]], axis=1)
    return jnp.pad(lon_padded, ((RATE, RATE), (0, 0), (0, 0)))

def tap_window(padded, tap_row, tap_col):
    return padded[tap_row * RATE:tap_row * RATE + H, tap_col * RATE:tap_col * RATE + W]

def reference(features, atrous_weight, norm_gain, norm_bias, head_weight, labels):
    total_cells = H * W
    padded = cycle_pad(features)
    summed = jnp.zeros((total_cells, COUT), jnp.float32)
    for tap_row in range(3):
        for tap_col in range(3):
            window = tap_window(padded, tap_row, tap_col).reshape(total_cells, CIN)
            summed = summed + jnp.dot(window, atrous_weight[tap_row, tap_col], preferred_element_type=jnp.float32)
    average = lax.optimization_barrier(jnp.sum(summed, 0)) / total_cells
    variance = lax.optimization_barrier(jnp.sum(summed * summed, 0)) / total_cells - average * average
    inverse = lax.rsqrt(variance + epsilon)
    normed = (summed - average) * inverse
    preact = norm_gain * normed + norm_bias
    hidden = jnp.maximum(preact, 0.0).astype(jnp.bfloat16)
    hidden_wide = hidden.astype(jnp.float32)
    logits = jnp.dot(hidden_wide, head_weight.T, precision=lax.Precision.HIGHEST)
    one_hot = (labels.reshape(total_cells)[:, None] == jnp.arange(CLASSES, dtype=jnp.int32)[None, :]).astype(jnp.float32)
    exponent = jnp.exp(logits)
    partition = lax.optimization_barrier(jnp.sum(exponent, 1, keepdims=True))
    mean_loss = jnp.sum(jnp.log(partition)[:, 0] - lax.optimization_barrier(jnp.sum(logits * one_hot, 1))) / total_cells
    grad_logits = exponent / partition - one_hot
    grad_head = jnp.dot(grad_logits.T, hidden_wide, precision=lax.Precision.HIGHEST) / total_cells
    d_hidden = jnp.dot(grad_logits, head_weight, precision=lax.Precision.HIGHEST)
    d_preact = jnp.where(preact > 0, d_hidden, 0.0)
    grad_bias = lax.optimization_barrier(jnp.sum(d_preact, 0)) / total_cells
    grad_gain = lax.optimization_barrier(jnp.sum(d_preact * normed, 0)) / total_cells
    d_summed = (norm_gain * inverse * (d_preact - grad_bias - normed * grad_gain)).astype(jnp.bfloat16)
    grad_padded = cycle_pad(d_summed.reshape(H, W, COUT))
    grad_acc = jnp.zeros((total_cells, CIN), jnp.float32)
    kernel_rows = []
    for tap_row in range(3):
        kernel_cols = []
        for tap_col in range(3):
            shifted = tap_window(grad_padded, 2 - tap_row, 2 - tap_col).reshape(total_cells, COUT)
            grad_acc = grad_acc + lax.dot_general(shifted, atrous_weight[tap_row, tap_col], (((1,), (1,)), ((), ())), preferred_element_type=jnp.float32)
            window = tap_window(padded, tap_row, tap_col).reshape(total_cells, CIN)
            kernel_cols.append(jnp.dot(window.T, d_summed, preferred_element_type=jnp.float32) / total_cells)
        kernel_rows.append(jnp.stack(kernel_cols, 1))
    grad_weight = jnp.stack(kernel_rows, 1)
    grad_features = grad_acc.astype(jnp.bfloat16).reshape(H, W, CIN)
    return (mean_loss, grad_features, grad_weight, grad_gain, grad_bias, grad_head)
```

```python
import jax
import jax.numpy as jnp
from jax import lax
from jax.experimental import pallas as pl
from jax.experimental.pallas import tpu as pltpu
from jax.sharding import PartitionSpec as P

RATE = 12
epsilon = 1e-05
BF = jnp.bfloat16
F32 = jnp.float32


def ring(x, axis, step, periodic):
    count = lax.axis_size(axis)
    pairs = [(i, (i + step) % count) for i in range(count)]
    if not periodic:
        pairs = [(i, i + step) for i in range(count) if 0 <= i + step < count]
    return lax.ppermute(x, axis, pairs)


def core_swap(x):
    count = lax.axis_size("lon")
    return lax.ppermute(x, "lon", [(i, i ^ 1) for i in range(count)])


def total(x):
    count = lax.axis_size("lat") * lax.axis_size("lon")
    spread = jnp.broadcast_to(x[None], (count,) + x.shape)
    return jnp.sum(lax.all_to_all(spread, ("lat", "lon"), 0, 0), 0)


def taps_forward(flat, weight, cols, height, breadth):
    cells, channels = flat.shape
    filters = weight.shape[2]
    step_rows = RATE * breadth
    ext = cells + 2 * step_rows
    first, stride = cols[0], (cols[1] - cols[0]) if len(cols) > 1 else 1

    def body(x_ref, w_ref, o_ref):
        r = pl.program_id(1)

        @pl.when(r == 0)
        def _():
            o_ref[...] = jnp.zeros_like(o_ref)

        part = jnp.dot(x_ref[...], w_ref[0], preferred_element_type=F32)
        at = pl.ds(pl.multiple_of((2 - r) * step_rows, step_rows), cells)
        o_ref[0, at, :] += part

    return pl.pallas_call(
        body,
        grid=(len(cols), 3),
        in_specs=[
            pl.BlockSpec((cells, channels), lambda c, r: (0, 0)),
            pl.BlockSpec((1, channels, filters), lambda c, r: (r * 3 + first + c * stride, 0, 0)),
        ],
        out_specs=pl.BlockSpec((1, ext, filters), lambda c, r: (c, 0, 0)),
        out_shape=jax.ShapeDtypeStruct((len(cols), ext, filters), F32),
        compiler_params=pltpu.CompilerParams(vmem_limit_bytes=48 * 1024 * 1024),
    )(flat, weight)


def grad_input(dcols, weight, cells, step_rows):
    channels, filters = weight.shape[1:]
    block = 512

    def body(d_ref, w_ref, o_ref):
        acc = None
        for r in range(3):
            for c in range(3):
                win = d_ref[2 - c, (2 - r) * step_rows : (2 - r) * step_rows + cells, :]
                part = lax.dot_general(
                    win, w_ref[r * 3 + c], (((1,), (1,)), ((), ())), preferred_element_type=F32
                )
                acc = part if acc is None else acc + part
        o_ref[...] = acc.astype(BF)

    return pl.pallas_call(
        body,
        grid=(channels // block,),
        in_specs=[
            pl.BlockSpec(dcols.shape, lambda n: (0, 0, 0)),
            pl.BlockSpec((9, block, filters), lambda n: (0, n, 0)),
        ],
        out_specs=pl.BlockSpec((cells, block), lambda n: (0, n)),
        out_shape=jax.ShapeDtypeStruct((cells, channels), BF),
        compiler_params=pltpu.CompilerParams(vmem_limit_bytes=48 * 1024 * 1024),
    )(dcols, weight)


def head(preact, labels, head_weight):
    hidden = jnp.maximum(preact, 0.0).astype(BF).astype(F32)
    logits = jnp.dot(hidden, head_weight.T, precision=lax.Precision.HIGHEST)
    classes = head_weight.shape[0]
    one_hot = (labels[:, None] == jnp.arange(classes, dtype=jnp.int32)[None, :]).astype(F32)
    exponent = jnp.exp(logits)
    partition = jnp.sum(exponent, 1, keepdims=True)
    grad_logits = exponent / partition - one_hot
    d_hidden = jnp.dot(grad_logits, head_weight, precision=lax.Precision.HIGHEST)
    d_preact = jnp.where(preact > 0, d_hidden, 0.0)
    return hidden, logits, one_hot, partition, grad_logits, d_preact


def shards(features, atrous_weight, norm_gain, norm_bias, head_weight, labels):
    height, breadth, channels = features.shape
    filters = atrous_weight.shape[3]
    classes = head_weight.shape[0]
    lats, lons = lax.axis_size("lat"), lax.axis_size("lon")
    lat = lax.axis_index("lat")
    core = lax.axis_index("lon") % 2
    cells = height * breadth
    total_cells = cells * lats * lons
    step_rows = RATE * breadth
    ext_rows = height + 2 * RATE
    weight = atrous_weight.reshape(9, channels, filters)
    flat = features.reshape(cells, channels)

    half = channels // (2 * lats)
    by_half = flat.reshape(cells, lats, 2, half)
    mine = lax.dynamic_index_in_dim(by_half, core, 2, False).reshape(cells, lats * half)
    other = lax.dynamic_index_in_dim(by_half, 1 - core, 2, False).reshape(cells, lats * half)
    theirs = core_swap(other)

    lab_w = ring(labels[:, breadth - RATE :], "lon", 1, True)
    lab_e = ring(labels[:, :RATE], "lon", -1, True)
    lab_row = jnp.concatenate([lab_w, labels, lab_e], 1)
    lab_n = ring(lab_row[height - RATE :], "lat", 1, False)
    lab_s = ring(lab_row[:RATE], "lat", -1, False)

    sides = taps_forward(flat, weight, (0, 2), height, breadth).reshape(2, ext_rows, breadth, filters)
    from_w = ring(sides[0, :, RATE:], "lon", 1, True)
    from_e = ring(sides[1, :, :RATE], "lon", -1, True)
    centre = taps_forward(flat, weight, (1,), height, breadth).reshape(ext_rows, breadth, filters)
    centre = centre + jnp.concatenate([sides[1, :, RATE:] + from_w, sides[0, :, :RATE] + from_e], 1)
    from_n = ring(centre[height + RATE :], "lat", 1, False)
    from_s = ring(centre[:RATE], "lat", -1, False)
    zero = jnp.zeros((height - RATE, breadth, filters), F32)
    summed = (
        centre[RATE : RATE + height]
        + jnp.concatenate([from_n, zero], 0)
        + jnp.concatenate([zero, from_s], 0)
    ).reshape(cells, filters)

    moments = total(jnp.stack([jnp.sum(summed, 0), jnp.sum(summed * summed, 0)]).reshape(-1, 128))
    moments = moments.reshape(2, filters)
    average = moments[0] / total_cells
    variance = moments[1] / total_cells - average * average
    inverse = lax.rsqrt(variance + epsilon)
    normed = (summed - average) * inverse
    preact = norm_gain * normed + norm_bias

    pre_low = preact.astype(BF).reshape(height, breadth, filters)
    pre_n = ring(pre_low[height - RATE :], "lat", 1, False)
    pre_s = ring(pre_low[:RATE], "lat", -1, False)
    pre_col = jnp.concatenate([pre_n, pre_low, pre_s], 0)
    pre_w = ring(pre_col[:, breadth - RATE :], "lon", 1, True)
    pre_e = ring(pre_col[:, :RATE], "lon", -1, True)

    hidden, logits, one_hot, partition, grad_logits, d_preact = head(preact, labels.reshape(-1), head_weight)
    loss_terms = jnp.sum(jnp.log(partition)[:, 0] - jnp.sum(logits * one_hot, 1))
    head_term = jnp.dot(grad_logits.T, hidden, precision=lax.Precision.HIGHEST)
    payload = jnp.concatenate(
        [
            jnp.sum(d_preact, 0)[None],
            jnp.sum(d_preact * normed, 0)[None],
            head_term,
            jnp.broadcast_to(loss_terms, (1, filters)),
        ],
        0,
    )
    totals = total(payload.reshape(-1, 128)).reshape(classes + 3, filters) / total_cells
    grad_bias, grad_gain, grad_head = totals[0], totals[1], totals[2 : 2 + classes]
    mean_loss = totals[2 + classes, 0]

    scale = norm_gain * inverse
    d_own = (scale * (d_preact - grad_bias - normed * grad_gain)).astype(BF)
    d_own = d_own.reshape(height, breadth, filters)

    def halo(pre, lab):
        shape = pre.shape
        wide = pre.reshape(-1, filters).astype(F32)
        d_pre = head(wide, lab.reshape(-1), head_weight)[-1]
        norm = (wide - norm_bias) / norm_gain
        return (scale * (d_pre - grad_bias - norm * grad_gain)).astype(BF).reshape(shape)

    has_n, has_s = lat > 0, lat < lats - 1
    side = RATE
    d_n = jnp.where(has_n, halo(pre_n, lab_n[:, side : side + breadth]), 0)
    d_s = jnp.where(has_s, halo(pre_s, lab_s[:, side : side + breadth]), 0)
    row = jnp.arange(ext_rows)[:, None, None]
    inside = ((row >= RATE) | has_n) & ((row < height + RATE) | has_s)
    lab_cols = jnp.concatenate([lab_n, lab_row, lab_s], 0)
    d_w = jnp.where(inside, halo(pre_w, lab_cols[:, :side]), 0)
    d_e = jnp.where(inside, halo(pre_e, lab_cols[:, side + breadth :]), 0)
    d_pad = jnp.concatenate([d_w, jnp.concatenate([d_n, d_own, d_s], 0), d_e], 1)
    d_pair = core_swap(d_pad)

    def columns(pad):
        parts = [pad[:, c * RATE : c * RATE + breadth].reshape(-1, filters) for c in range(3)]
        return jnp.stack(parts, 0)

    d_cols = columns(d_pad)
    d_cols_pair = columns(d_pair)

    def windows(cols):
        return jnp.stack(
            [
                cols[2 - c, (2 - r) * step_rows : (2 - r) * step_rows + cells]
                for r in range(3)
                for c in range(3)
            ],
            0,
        )

    shifted = jnp.concatenate([windows(d_cols), windows(d_cols_pair)], 1)
    pair_in = jnp.concatenate([mine, theirs], 0)
    partial = jnp.einsum("tqf,qc->tfc", shifted, pair_in, preferred_element_type=F32).astype(BF)
    own_f = filters // lons
    blocks = partial.reshape(9, lons, own_f, lats, half)
    blocks = jnp.transpose(blocks, (3, 1, 0, 2, 4)).reshape(lats * lons, 9, own_f, half)
    got = lax.all_to_all(blocks, ("lat", "lon"), 0, 0)
    got = got.reshape(lats * lons // 2, 2, 9, own_f, half)
    weight_block = jnp.sum(got.astype(F32), 0) / total_cells
    grad_weight = jnp.transpose(weight_block, (0, 3, 1, 2)).reshape(2 * half, 3, 3, own_f)

    grad_features = grad_input(d_cols, weight, cells, step_rows).reshape(height, breadth, channels)
    return (mean_loss, grad_features, grad_weight, grad_gain, grad_bias, grad_head)


def solution(mesh):
    return jax.shard_map(
        shards,
        mesh=mesh,
        in_specs=(P("lat", "lon", None), P(), P(), P(), P(), P("lat", "lon")),
        out_specs=(P(), P("lat", "lon", None), P("lat", None, None, "lon"), P(), P(), P()),
        check_vma=False,
    )
```

```python
import jax
import jax.numpy as jnp
from jax import lax
from jax.experimental import pallas as pl
from jax.experimental.pallas import tpu as pltpu
from jax.sharding import PartitionSpec as P

RATE = 12
epsilon = 1e-05
BF = jnp.bfloat16
F32 = jnp.float32


def ring(x, axis, step, periodic):
    count = lax.axis_size(axis)
    pairs = [(i, (i + step) % count) for i in range(count)]
    if not periodic:
        pairs = [(i, i + step) for i in range(count) if 0 <= i + step < count]
    return lax.ppermute(x, axis, pairs)


def core_swap(x):
    count = lax.axis_size("lon")
    return lax.ppermute(x, "lon", [(i, i ^ 1) for i in range(count)])


def total(x):
    count = lax.axis_size("lat") * lax.axis_size("lon")
    spread = jnp.broadcast_to(x[None], (count,) + x.shape)
    return jnp.sum(lax.all_to_all(spread, ("lat", "lon"), 0, 0), 0)


def outer_rows(flat, weight, edge):
    cells, channels = flat.shape
    filters = weight.shape[2]

    def body(x_ref, w_ref, o_ref):
        at = pl.ds(pl.multiple_of(pl.program_id(0) * (cells - edge), 16), edge)
        o_ref[0, 0] = jnp.dot(x_ref[at, :], w_ref[0], preferred_element_type=F32)

    return pl.pallas_call(
        body,
        grid=(2, 3),
        in_specs=[
            pl.BlockSpec((cells, channels), lambda e, c: (0, 0)),
            pl.BlockSpec((1, channels, filters), lambda e, c: ((1 - e) * 6 + c, 0, 0)),
        ],
        out_specs=pl.BlockSpec((1, 1, edge, filters), lambda e, c: (e, c, 0, 0)),
        out_shape=jax.ShapeDtypeStruct((2, 3, edge, filters), F32),
        compiler_params=pltpu.CompilerParams(vmem_limit_bytes=48 * 1024 * 1024),
    )(flat, weight)


def inner_rows(flat, weight, edge, cols):
    cells, channels = flat.shape
    filters = weight.shape[2]
    first, stride = cols[0], (cols[1] - cols[0]) if len(cols) > 1 else 1

    def body(x_ref, w_ref, o_ref):
        k = pl.program_id(1)

        @pl.when(k == 0)
        def _():
            o_ref[0] = jnp.dot(x_ref[...], w_ref[0], preferred_element_type=F32)

        @pl.when(k == 1)
        def _():
            o_ref[0, edge:, :] += jnp.dot(x_ref[: cells - edge, :], w_ref[0], preferred_element_type=F32)

        @pl.when(k == 2)
        def _():
            o_ref[0, : cells - edge, :] += jnp.dot(x_ref[edge:, :], w_ref[0], preferred_element_type=F32)

    def tap(c, k):
        return ((k * k * 3 - k * 5 + 2) // 2 * 3 + first + c * stride, 0, 0)

    return pl.pallas_call(
        body,
        grid=(len(cols), 3),
        in_specs=[
            pl.BlockSpec((cells, channels), lambda c, k: (0, 0)),
            pl.BlockSpec((1, channels, filters), tap),
        ],
        out_specs=pl.BlockSpec((1, cells, filters), lambda c, k: (c, 0, 0)),
        out_shape=jax.ShapeDtypeStruct((len(cols), cells, filters), F32),
        compiler_params=pltpu.CompilerParams(vmem_limit_bytes=48 * 1024 * 1024),
    )(flat, weight)


def split_halves(flat, which, half):
    cells, channels = flat.shape
    count = channels // (2 * half)

    def body(which_ref, x_ref, mine_ref, other_ref):
        low, high = x_ref[:, :half], x_ref[:, half:]
        first = which_ref[0] == 0

        @pl.when(first)
        def _():
            mine_ref[...] = low
            other_ref[...] = high

        @pl.when(jnp.logical_not(first))
        def _():
            mine_ref[...] = high
            other_ref[...] = low

    shape = jax.ShapeDtypeStruct((cells, count * half), BF)
    block = pl.BlockSpec((cells, half), lambda i, w: (0, i))
    return pl.pallas_call(
        body,
        grid_spec=pltpu.PrefetchScalarGridSpec(
            num_scalar_prefetch=1,
            grid=(count,),
            in_specs=[pl.BlockSpec((cells, 2 * half), lambda i, w: (0, i))],
            out_specs=[block, block],
        ),
        out_shape=[shape, shape],
    )(which.reshape(1).astype(jnp.int32), flat)


def grad_input(dcols, weight, cells, step_rows):
    channels, filters = weight.shape[1:]
    block = 512

    def body(d_ref, w_ref, o_ref):
        acc = None
        for r in range(3):
            for c in range(3):
                win = d_ref[2 - c, (2 - r) * step_rows : (2 - r) * step_rows + cells, :]
                part = lax.dot_general(
                    win, w_ref[r * 3 + c], (((1,), (1,)), ((), ())), preferred_element_type=F32
                )
                acc = part if acc is None else acc + part
        o_ref[...] = acc.astype(BF)

    return pl.pallas_call(
        body,
        grid=(channels // block,),
        in_specs=[
            pl.BlockSpec(dcols.shape, lambda n: (0, 0, 0)),
            pl.BlockSpec((9, block, filters), lambda n: (0, n, 0)),
        ],
        out_specs=pl.BlockSpec((cells, block), lambda n: (0, n)),
        out_shape=jax.ShapeDtypeStruct((cells, channels), BF),
        compiler_params=pltpu.CompilerParams(vmem_limit_bytes=48 * 1024 * 1024),
    )(dcols, weight)


def head(preact, labels, head_weight):
    hidden = jnp.maximum(preact, 0.0).astype(BF).astype(F32)
    logits = jnp.dot(hidden, head_weight.T, precision=lax.Precision.HIGHEST)
    classes = head_weight.shape[0]
    one_hot = (labels[:, None] == jnp.arange(classes, dtype=jnp.int32)[None, :]).astype(F32)
    exponent = jnp.exp(logits)
    partition = jnp.sum(exponent, 1, keepdims=True)
    grad_logits = exponent / partition - one_hot
    d_hidden = jnp.dot(grad_logits, head_weight, precision=lax.Precision.HIGHEST)
    d_preact = jnp.where(preact > 0, d_hidden, 0.0)
    return hidden, logits, one_hot, partition, grad_logits, d_preact


def shards(features, atrous_weight, norm_gain, norm_bias, head_weight, labels):
    height, breadth, channels = features.shape
    filters = atrous_weight.shape[3]
    classes = head_weight.shape[0]
    lats, lons = lax.axis_size("lat"), lax.axis_size("lon")
    core = lax.axis_index("lon") % 2
    cells = height * breadth
    total_cells = cells * lats * lons
    step_rows = RATE * breadth
    weight = atrous_weight.reshape(9, channels, filters)
    flat = features.reshape(cells, channels)

    rest = breadth - RATE
    outer = outer_rows(flat, weight, step_rows).reshape(2, 3, RATE, breadth, filters)
    outer_w = ring(outer[:, 0, :, RATE:], "lon", 1, True)
    outer_e = ring(outer[:, 2, :, :rest], "lon", -1, True)
    sides = inner_rows(flat, weight, step_rows, (0, 2)).reshape(2, height, breadth, filters)
    inner_w = ring(sides[0, :, RATE:], "lon", 1, True)
    inner_e = ring(sides[1, :, :rest], "lon", -1, True)
    strips = outer[:, 1] + jnp.concatenate(
        [outer[:, 2, :, rest:] + outer_w, outer[:, 0, :, :RATE] + outer_e], 2
    )
    from_s = ring(strips[0], "lat", -1, False)
    from_n = ring(strips[1], "lat", 1, False)
    centre = inner_rows(flat, weight, step_rows, (1,)).reshape(height, breadth, filters)
    centre = centre + jnp.concatenate([sides[1, :, rest:] + inner_w, sides[0, :, :RATE] + inner_e], 1)

    half = channels // (2 * lats)
    mine, other = split_halves(flat, core, half)
    theirs = core_swap(other)

    zero = jnp.zeros((height - RATE, breadth, filters), F32)
    summed = (
        centre + jnp.concatenate([from_n, zero], 0) + jnp.concatenate([zero, from_s], 0)
    ).reshape(cells, filters)

    moments = total(jnp.stack([jnp.sum(summed, 0), jnp.sum(summed * summed, 0)]).reshape(-1, 128))
    moments = moments.reshape(2, filters)
    average = moments[0] / total_cells
    variance = moments[1] / total_cells - average * average
    inverse = lax.rsqrt(variance + epsilon)
    normed = (summed - average) * inverse
    preact = norm_gain * normed + norm_bias

    hidden, logits, one_hot, partition, grad_logits, d_preact = head(preact, labels.reshape(-1), head_weight)
    loss_terms = jnp.sum(jnp.log(partition)[:, 0] - jnp.sum(logits * one_hot, 1))
    head_term = jnp.dot(grad_logits.T, hidden, precision=lax.Precision.HIGHEST)
    payload = jnp.concatenate(
        [
            jnp.sum(d_preact, 0)[None],
            jnp.sum(d_preact * normed, 0)[None],
            head_term,
            jnp.broadcast_to(loss_terms, (1, filters)),
        ],
        0,
    )
    totals = total(payload.reshape(-1, 4, 128)).reshape(classes + 3, filters) / total_cells
    grad_bias, grad_gain, grad_head = totals[0], totals[1], totals[2 : 2 + classes]
    mean_loss = totals[2 + classes, 0]

    scale = norm_gain * inverse
    d_own = (scale * (d_preact - grad_bias - normed * grad_gain)).astype(BF)
    d_own = d_own.reshape(height, breadth, filters)

    d_n = ring(d_own[height - RATE :], "lat", 1, False)
    d_s = ring(d_own[:RATE], "lat", -1, False)
    d_col = jnp.concatenate([d_n, d_own, d_s], 0)
    d_w = ring(d_col[:, breadth - RATE :], "lon", 1, True)
    d_e = ring(d_col[:, :RATE], "lon", -1, True)
    d_pad = jnp.concatenate([d_w, d_col, d_e], 1)
    d_pair = core_swap(d_pad)

    def columns(pad):
        parts = [pad[:, c * RATE : c * RATE + breadth].reshape(-1, filters) for c in range(3)]
        return jnp.stack(parts, 0)

    d_cols = columns(d_pad)
    d_cols_pair = columns(d_pair)

    def windows(cols):
        return jnp.stack(
            [
                cols[2 - c, (2 - r) * step_rows : (2 - r) * step_rows + cells]
                for r in range(3)
                for c in range(3)
            ],
            0,
        )

    shifted = jnp.concatenate([windows(d_cols), windows(d_cols_pair)], 1)
    pair_in = jnp.concatenate([mine, theirs], 0)
    partial = jnp.einsum("tqf,qc->tfc", shifted, pair_in, preferred_element_type=F32).astype(BF)
    own_f = filters // lons
    blocks = partial.reshape(9, lons, own_f, lats, half)
    blocks = jnp.transpose(blocks, (3, 1, 0, 2, 4)).reshape(lats * lons, 9, own_f, half)
    got = lax.all_to_all(blocks, ("lat", "lon"), 0, 0)
    got = got.reshape(lats * lons // 2, 2, 9, own_f, half)
    weight_block = jnp.sum(got.astype(F32), 0) / total_cells
    grad_weight = jnp.transpose(weight_block, (0, 3, 1, 2)).reshape(2 * half, 3, 3, own_f)

    grad_features = grad_input(d_cols, weight, cells, step_rows).reshape(height, breadth, channels)
    return (mean_loss, grad_features, grad_weight, grad_gain, grad_bias, grad_head)


def solution(mesh):
    return jax.shard_map(
        shards,
        mesh=mesh,
        in_specs=(P("lat", "lon", None), P(), P(), P(), P(), P("lat", "lon")),
        out_specs=(P(), P("lat", "lon", None), P("lat", None, None, "lon"), P(), P(), P()),
        check_vma=False,
    )
```

```python
import jax
import jax.numpy as jnp
from jax import lax
from jax.experimental import pallas as pl
from jax.experimental.pallas import tpu as pltpu
from jax.sharding import PartitionSpec as P

RATE = 12
epsilon = 1e-05
BF = jnp.bfloat16
F32 = jnp.float32


def ring(x, axis, step, periodic):
    count = lax.axis_size(axis)
    pairs = [(i, (i + step) % count) for i in range(count)]
    if not periodic:
        pairs = [(i, i + step) for i in range(count) if 0 <= i + step < count]
    return lax.ppermute(x, axis, pairs)


def swap(x, mask):
    count = lax.axis_size("lon")
    return lax.ppermute(x, "lon", [(i, i ^ mask) for i in range(count)])


def to_groups(x, gap):
    count = lax.axis_size("lon")
    pairs = []
    for first in range(0, count, 4):
        pairs.append((first + 3, (first + 3 + gap) % count))
        pairs.append((first, (first - gap) % count))
    return lax.ppermute(x, "lon", pairs)


def total(x):
    count = lax.axis_size("lat") * lax.axis_size("lon")
    spread = jnp.broadcast_to(x[None], (count,) + x.shape)
    return jnp.sum(lax.all_to_all(spread, ("lat", "lon"), 0, 0), 0)


def outer_rows(flat, weight, edge):
    cells, channels = flat.shape
    filters = weight.shape[2]

    def body(x_ref, w_ref, o_ref):
        at = pl.ds(pl.multiple_of(pl.program_id(0) * (cells - edge), 16), edge)
        o_ref[0, 0] = jnp.dot(x_ref[at, :], w_ref[0], preferred_element_type=F32)

    return pl.pallas_call(
        body,
        grid=(2, 3),
        in_specs=[
            pl.BlockSpec((cells, channels), lambda e, c: (0, 0)),
            pl.BlockSpec((1, channels, filters), lambda e, c: ((1 - e) * 6 + c, 0, 0)),
        ],
        out_specs=pl.BlockSpec((1, 1, edge, filters), lambda e, c: (e, c, 0, 0)),
        out_shape=jax.ShapeDtypeStruct((2, 3, edge, filters), F32),
        compiler_params=pltpu.CompilerParams(vmem_limit_bytes=48 * 1024 * 1024),
    )(flat, weight)


def inner_rows(flat, weight, edge, cols):
    cells, channels = flat.shape
    filters = weight.shape[2]
    first, stride = cols[0], (cols[1] - cols[0]) if len(cols) > 1 else 1

    def body(x_ref, w_ref, o_ref):
        k = pl.program_id(1)

        @pl.when(k == 0)
        def _():
            o_ref[0] = jnp.dot(x_ref[...], w_ref[0], preferred_element_type=F32)

        @pl.when(k == 1)
        def _():
            o_ref[0, edge:, :] += jnp.dot(x_ref[: cells - edge, :], w_ref[0], preferred_element_type=F32)

        @pl.when(k == 2)
        def _():
            o_ref[0, : cells - edge, :] += jnp.dot(x_ref[edge:, :], w_ref[0], preferred_element_type=F32)

    def tap(c, k):
        return ((k * k * 3 - k * 5 + 2) // 2 * 3 + first + c * stride, 0, 0)

    return pl.pallas_call(
        body,
        grid=(len(cols), 3),
        in_specs=[
            pl.BlockSpec((cells, channels), lambda c, k: (0, 0)),
            pl.BlockSpec((1, channels, filters), tap),
        ],
        out_specs=pl.BlockSpec((1, cells, filters), lambda c, k: (c, 0, 0)),
        out_shape=jax.ShapeDtypeStruct((len(cols), cells, filters), F32),
        compiler_params=pltpu.CompilerParams(vmem_limit_bytes=48 * 1024 * 1024),
    )(flat, weight)


def split_quarters(flat, where, quarter):
    cells, channels = flat.shape
    blocks = channels // (4 * quarter)

    def body(where_ref, x_ref, *o_refs):
        parts = []
        for t in range(4):
            left = x_ref[:, t * quarter : (t + 1) * quarter]
            right = x_ref[:, (4 + t) * quarter : (5 + t) * quarter]
            parts.append(jnp.concatenate([left, right], 1).T)
        for here in range(4):

            @pl.when(where_ref[0] == here)
            def _():
                for t in range(4):
                    o_refs[here ^ t][...] = parts[t]

    return pl.pallas_call(
        body,
        grid_spec=pltpu.PrefetchScalarGridSpec(
            num_scalar_prefetch=1,
            grid=(blocks // 2,),
            in_specs=[pl.BlockSpec((cells, 8 * quarter), lambda i, w: (0, i))],
            out_specs=[pl.BlockSpec((2 * quarter, cells), lambda i, w: (i, 0))] * 4,
        ),
        out_shape=[jax.ShapeDtypeStruct((blocks * quarter, cells), BF)] * 4,
        compiler_params=pltpu.CompilerParams(vmem_limit_bytes=48 * 1024 * 1024),
    )(where.reshape(1).astype(jnp.int32), flat)


def group_windows(place, mine, pair, breadth):
    rows, _, filters = mine[0].shape
    step, lead = 8, 16
    wide = lead + 4 * breadth + lead

    def body(place_ref, *refs):
        parts, o_ref, buf = refs[:8], refs[8], refs[9]
        here = place_ref[0]
        order = (0, 4, 1, 5)
        for k in range(4):
            first = pl.multiple_of(lead + breadth * (here ^ k), 8)
            d = parts[order[k]][...]
            o_ref[1, k] = d.reshape(step * breadth, filters)
            buf[:, pl.ds(first, breadth), :] = d.astype(F32)
        ends = (here == 0) | (here == 3)
        west = here < 2
        near, far = [jnp.where(ends, parts[n][...], parts[4 + n][...]).astype(F32) for n in (2, 3)]
        buf[:, lead - RATE : lead, :] = jnp.where(west, near, far)
        buf[:, lead + 4 * breadth : lead + 4 * breadth + RATE, :] = jnp.where(west, far, near)
        for t in range(4):
            for c in (0, 2):
                first = lead + t * breadth + (c - 1) * RATE
                win = buf[:, first : first + breadth, :]
                o_ref[c, here ^ t] = win.reshape(step * breadth, filters).astype(BF)

    arrays = tuple(mine) + tuple(pair)
    return pl.pallas_call(
        body,
        grid_spec=pltpu.PrefetchScalarGridSpec(
            num_scalar_prefetch=1,
            grid=(rows // step,),
            in_specs=[
                pl.BlockSpec((step, x.shape[1], filters), lambda i, place: (i, 0, 0)) for x in arrays
            ],
            out_specs=pl.BlockSpec((3, 4, step * breadth, filters), lambda i, place: (0, 0, i, 0)),
            scratch_shapes=[pltpu.VMEM((step, wide, filters), F32)],
        ),
        out_shape=jax.ShapeDtypeStruct((3, 4, rows * breadth, filters), BF),
        compiler_params=pltpu.CompilerParams(vmem_limit_bytes=48 * 1024 * 1024),
    )(place.reshape(1).astype(jnp.int32), *arrays)


def grad_kernel(d_all, group_in, lats, lons, step_rows):
    filters = d_all.shape[3]
    width, cells = group_in[0].shape
    quarter = width // lats
    half_f = filters // lons // 2

    def body(d_ref, *refs):
        x_refs, o_ref = refs[:4], refs[4]
        for r in range(3):
            at = (2 - r) * step_rows
            acc = None
            for k in range(4):
                part = jnp.dot(x_refs[k][...], d_ref[0, k, at : at + cells, :], preferred_element_type=F32)
                acc = part if acc is None else acc + part
            out = acc.T
            for pair in range(lats // 2):
                both = out[:, pair * 2 * quarter : (pair + 1) * 2 * quarter]
                both = both.reshape(lons, 2, half_f, 2 * quarter)
                low, high = both[:, 0], both[:, 1]
                even = jnp.concatenate([low[..., :quarter], high[..., :quarter]], 2)
                odd = jnp.concatenate([low[..., quarter:], high[..., quarter:]], 2)
                o_ref[2 * pair, :, r, 0] = even.astype(BF)
                o_ref[2 * pair + 1, :, r, 0] = odd.astype(BF)

    return pl.pallas_call(
        body,
        grid=(3,),
        in_specs=[
            pl.BlockSpec((1,) + d_all.shape[1:], lambda c: (2 - c, 0, 0, 0)),
        ]
        + [pl.BlockSpec((width, cells), lambda c: (0, 0))] * 4,
        out_specs=pl.BlockSpec((lats, lons, 3, 1, half_f, 2 * quarter), lambda c: (0, 0, 0, c, 0, 0)),
        out_shape=jax.ShapeDtypeStruct((lats, lons, 3, 3, half_f, 2 * quarter), BF),
        compiler_params=pltpu.CompilerParams(vmem_limit_bytes=56 * 1024 * 1024),
    )(d_all, *group_in)


def grad_input(dcols, weight, cells, step_rows):
    channels, filters = weight.shape[1:]
    block = 512

    def body(d_ref, w_ref, o_ref):
        acc = None
        for r in range(3):
            for c in range(3):
                win = d_ref[2 - c, (2 - r) * step_rows : (2 - r) * step_rows + cells, :]
                part = lax.dot_general(
                    win, w_ref[r * 3 + c], (((1,), (1,)), ((), ())), preferred_element_type=F32
                )
                acc = part if acc is None else acc + part
        o_ref[...] = acc.astype(BF)

    return pl.pallas_call(
        body,
        grid=(channels // block,),
        in_specs=[
            pl.BlockSpec(dcols.shape, lambda n: (0, 0, 0)),
            pl.BlockSpec((9, block, filters), lambda n: (0, n, 0)),
        ],
        out_specs=pl.BlockSpec((cells, block), lambda n: (0, n)),
        out_shape=jax.ShapeDtypeStruct((cells, channels), BF),
        compiler_params=pltpu.CompilerParams(vmem_limit_bytes=48 * 1024 * 1024),
    )(dcols, weight)


def head(preact, labels, head_weight):
    hidden = jnp.maximum(preact, 0.0).astype(BF).astype(F32)
    logits = jnp.dot(hidden, head_weight.T, precision=lax.Precision.HIGHEST)
    classes = head_weight.shape[0]
    one_hot = (labels[:, None] == jnp.arange(classes, dtype=jnp.int32)[None, :]).astype(F32)
    exponent = jnp.exp(logits)
    partition = jnp.sum(exponent, 1, keepdims=True)
    grad_logits = exponent / partition - one_hot
    d_hidden = jnp.dot(grad_logits, head_weight, precision=lax.Precision.HIGHEST)
    d_preact = jnp.where(preact > 0, d_hidden, 0.0)
    return hidden, logits, one_hot, partition, grad_logits, d_preact


def shards(features, atrous_weight, norm_gain, norm_bias, head_weight, labels):
    height, breadth, channels = features.shape
    filters = atrous_weight.shape[3]
    classes = head_weight.shape[0]
    lats, lons = lax.axis_size("lat"), lax.axis_size("lon")
    lat = lax.axis_index("lat")
    place = lax.axis_index("lon") % 4
    cells = height * breadth
    total_cells = cells * lats * lons
    step_rows = RATE * breadth
    weight = atrous_weight.reshape(9, channels, filters)
    flat = features.reshape(cells, channels)

    rest = breadth - RATE
    outer = outer_rows(flat, weight, step_rows).reshape(2, 3, RATE, breadth, filters)
    outer, late_weight = lax.optimization_barrier((outer, weight))
    outer_w = ring(outer[:, 0, :, RATE:], "lon", 1, True)
    outer_e = ring(outer[:, 2, :, :rest], "lon", -1, True)
    sides = inner_rows(flat, late_weight, step_rows, (0, 2)).reshape(2, height, breadth, filters)
    inner_w = ring(sides[0, :, RATE:], "lon", 1, True)
    inner_e = ring(sides[1, :, :rest], "lon", -1, True)
    strips = outer[:, 1] + jnp.concatenate(
        [outer[:, 2, :, rest:] + outer_w, outer[:, 0, :, :RATE] + outer_e], 2
    )
    from_s = ring(strips[0], "lat", -1, False)
    from_n = ring(strips[1], "lat", 1, False)
    quarter = channels // (4 * lats)
    quarters = split_quarters(flat, place, quarter)
    inner_w, inner_e, quarters = lax.optimization_barrier((inner_w, inner_e, quarters))
    group_in = [quarters[0]] + [swap(quarters[k], k) for k in range(1, 4)]

    centre = inner_rows(flat, late_weight, step_rows, (1,)).reshape(height, breadth, filters)
    centre = centre + jnp.concatenate([sides[1, :, rest:] + inner_w, sides[0, :, :RATE] + inner_e], 1)

    zero = jnp.zeros((height - RATE, breadth, filters), F32)
    summed = (
        centre + jnp.concatenate([from_n, zero], 0) + jnp.concatenate([zero, from_s], 0)
    ).reshape(cells, filters)

    moments = total(jnp.stack([jnp.sum(summed, 0), jnp.sum(summed * summed, 0)]).reshape(-1, 128))
    moments, group_in[2] = lax.optimization_barrier((moments, group_in[2]))
    moments = moments.reshape(2, filters)
    average = moments[0] / total_cells
    variance = moments[1] / total_cells - average * average
    inverse = lax.rsqrt(variance + epsilon)
    normed = (summed - average) * inverse
    preact = norm_gain * normed + norm_bias

    pre_low = preact.astype(BF).reshape(height, breadth, filters)
    lab_low = labels.T.astype(BF)

    def with_labels(rows):
        lab = jnp.pad(lab_low[:, rows], ((0, 0), (0, filters - RATE)))
        return jnp.concatenate([pre_low[rows], lab[None]], 0)

    pre_n = ring(with_labels(slice(height - RATE, height)), "lat", 1, False)
    pre_s = ring(with_labels(slice(0, RATE)), "lat", -1, False)

    hidden, logits, one_hot, partition, grad_logits, d_preact = head(preact, labels.reshape(-1), head_weight)
    loss_terms = jnp.sum(jnp.log(partition)[:, 0] - jnp.sum(logits * one_hot, 1))
    head_term = jnp.dot(grad_logits.T, hidden, precision=lax.Precision.HIGHEST)
    payload = jnp.concatenate(
        [
            jnp.sum(d_preact, 0)[None],
            jnp.sum(d_preact * normed, 0)[None],
            head_term,
            jnp.broadcast_to(loss_terms, (1, filters)),
        ],
        0,
    )
    totals = total(payload.reshape(-1, 4, 128))
    totals, group_in[3] = lax.optimization_barrier((totals, group_in[3]))
    totals = totals.reshape(classes + 3, filters) / total_cells
    grad_bias, grad_gain, grad_head = totals[0], totals[1], totals[2 : 2 + classes]
    mean_loss = totals[2 + classes, 0]

    scale = norm_gain * inverse
    slope = inverse * grad_gain
    shift = slope * norm_bias - scale * grad_bias
    d_own = (scale * (d_preact - grad_bias - normed * grad_gain)).astype(BF)

    def halo(pre, exists):
        lab = pre[RATE, :, :RATE].T.astype(jnp.int32)
        wide = pre[:RATE].astype(F32).reshape(step_rows, filters)
        d_pre = head(wide, lab.reshape(step_rows), head_weight)[-1]
        d = scale * d_pre - slope * wide + shift
        return jnp.where(exists, d, 0.0).astype(BF)

    d_col = jnp.concatenate([halo(pre_n, lat > 0), d_own, halo(pre_s, lat < lats - 1)], 0)
    d_col = d_col.reshape(height + 2 * RATE, breadth, filters)
    strip = jnp.where(place == 0, d_col[:, :RATE], d_col[:, breadth - RATE :])
    mine = (d_col, swap(d_col, 2), to_groups(strip, 1), to_groups(strip, 4))
    pair = [swap(x, 1) for x in mine]
    d_all = group_windows(place, mine, pair, breadth)

    blocks = grad_kernel(d_all, group_in, lats, lons, step_rows)
    blocks = blocks.reshape(lats * lons, -1, 2 * quarter)
    got = lax.all_to_all(blocks, ("lat", "lon"), 0, 0)
    own_f = filters // lons
    got = got.reshape(lats, lons // 4, 4, -1, 2 * quarter)
    weight_block = jnp.sum(got.astype(F32), (0, 1)) / total_cells
    weight_block = weight_block.reshape(4, 9, own_f // 2, 2, quarter)
    grad_weight = jnp.transpose(weight_block, (0, 4, 1, 3, 2)).reshape(4 * quarter, 3, 3, own_f)

    grad_features = grad_input(d_all[:, 0], weight, cells, step_rows).reshape(height, breadth, channels)
    return (mean_loss, grad_features, grad_weight, grad_gain, grad_bias, grad_head)


def solution(mesh):
    return jax.shard_map(
        shards,
        mesh=mesh,
        in_specs=(P("lat", "lon", None), P(), P(), P(), P(), P("lat", "lon")),
        out_specs=(P(), P("lat", "lon", None), P("lat", None, None, "lon"), P(), P(), P()),
        check_vma=False,
    )
```

```python
import jax
import jax.numpy as jnp
from jax import lax
from jax.experimental import pallas as pl
from jax.experimental.pallas import tpu as pltpu
from jax.sharding import PartitionSpec as P

RATE = 12
epsilon = 1e-05
BF = jnp.bfloat16
F32 = jnp.float32


def ring(x, axis, step, periodic):
    count = lax.axis_size(axis)
    pairs = [(i, (i + step) % count) for i in range(count)]
    if not periodic:
        pairs = [(i, i + step) for i in range(count) if 0 <= i + step < count]
    return lax.ppermute(x, axis, pairs)


def swap(x, mask):
    count = lax.axis_size("lon")
    return lax.ppermute(x, "lon", [(i, i ^ mask) for i in range(count)])


def to_groups(x, gap):
    count = lax.axis_size("lon")
    pairs = []
    for first in range(0, count, 4):
        pairs.append((first + 3, (first + 3 + gap) % count))
        pairs.append((first, (first - gap) % count))
    return lax.ppermute(x, "lon", pairs)


def total(x):
    count = lax.axis_size("lat") * lax.axis_size("lon")
    groups = [list(range(core, count, 2)) for core in range(2)]
    x = x + swap(x, 1)
    spread = jnp.broadcast_to(x[None], (count // 2,) + x.shape)
    return jnp.sum(lax.all_to_all(spread, ("lat", "lon"), 0, 0, axis_index_groups=groups), 0)


def outer_rows(flat, weight, edge):
    cells, channels = flat.shape
    filters = weight.shape[2]

    def body(x_ref, w_ref, o_ref):
        at = pl.ds(pl.multiple_of(pl.program_id(0) * (cells - edge), 16), edge)
        o_ref[0, 0] = jnp.dot(x_ref[at, :], w_ref[0], preferred_element_type=F32)

    return pl.pallas_call(
        body,
        grid=(2, 3),
        in_specs=[
            pl.BlockSpec((cells, channels), lambda e, c: (0, 0)),
            pl.BlockSpec((1, channels, filters), lambda e, c: ((1 - e) * 6 + c, 0, 0)),
        ],
        out_specs=pl.BlockSpec((1, 1, edge, filters), lambda e, c: (e, c, 0, 0)),
        out_shape=jax.ShapeDtypeStruct((2, 3, edge, filters), F32),
        compiler_params=pltpu.CompilerParams(vmem_limit_bytes=48 * 1024 * 1024),
    )(flat, weight)


def inner_rows(flat, weight, edge, cols):
    cells, channels = flat.shape
    filters = weight.shape[2]
    first, stride = cols[0], (cols[1] - cols[0]) if len(cols) > 1 else 1

    def body(x_ref, w_ref, o_ref):
        k = pl.program_id(1)

        @pl.when(k == 0)
        def _():
            o_ref[0] = jnp.dot(x_ref[...], w_ref[0], preferred_element_type=F32)

        @pl.when(k == 1)
        def _():
            o_ref[0, edge:, :] += jnp.dot(x_ref[: cells - edge, :], w_ref[0], preferred_element_type=F32)

        @pl.when(k == 2)
        def _():
            o_ref[0, : cells - edge, :] += jnp.dot(x_ref[edge:, :], w_ref[0], preferred_element_type=F32)

    def tap(c, k):
        return ((k * k * 3 - k * 5 + 2) // 2 * 3 + first + c * stride, 0, 0)

    return pl.pallas_call(
        body,
        grid=(len(cols), 3),
        in_specs=[
            pl.BlockSpec((cells, channels), lambda c, k: (0, 0)),
            pl.BlockSpec((1, channels, filters), tap),
        ],
        out_specs=pl.BlockSpec((1, cells, filters), lambda c, k: (c, 0, 0)),
        out_shape=jax.ShapeDtypeStruct((len(cols), cells, filters), F32),
        compiler_params=pltpu.CompilerParams(vmem_limit_bytes=48 * 1024 * 1024),
    )(flat, weight)


def split_quarters(flat, where, quarter):
    cells, channels = flat.shape
    blocks = channels // (4 * quarter)

    def body(where_ref, x_ref, *o_refs):
        parts = []
        for t in range(4):
            left = x_ref[:, t * quarter : (t + 1) * quarter]
            right = x_ref[:, (4 + t) * quarter : (5 + t) * quarter]
            parts.append(jnp.concatenate([left, right], 1).T)
        for here in range(4):

            @pl.when(where_ref[0] == here)
            def _():
                for t in range(4):
                    o_refs[here ^ t][...] = parts[t]

    return pl.pallas_call(
        body,
        grid_spec=pltpu.PrefetchScalarGridSpec(
            num_scalar_prefetch=1,
            grid=(blocks // 2,),
            in_specs=[pl.BlockSpec((cells, 8 * quarter), lambda i, w: (0, i))],
            out_specs=[pl.BlockSpec((2 * quarter, cells), lambda i, w: (i, 0))] * 4,
        ),
        out_shape=[jax.ShapeDtypeStruct((blocks * quarter, cells), BF)] * 4,
        compiler_params=pltpu.CompilerParams(vmem_limit_bytes=48 * 1024 * 1024),
    )(where.reshape(1).astype(jnp.int32), flat)


def group_windows(place, mine, pair, breadth):
    rows, _, filters = mine[0].shape
    step, lead = 8, 16
    wide = lead + 4 * breadth + lead

    def body(place_ref, *refs):
        parts, o_ref, buf = refs[:8], refs[8], refs[9]
        here = place_ref[0]
        order = (0, 4, 1, 5)
        for k in range(4):
            first = pl.multiple_of(lead + breadth * (here ^ k), 8)
            d = parts[order[k]][...]
            o_ref[1, k] = d.reshape(step * breadth, filters)
            buf[:, pl.ds(first, breadth), :] = d.astype(F32)
        ends = (here == 0) | (here == 3)
        west = here < 2
        near, far = [jnp.where(ends, parts[n][...], parts[4 + n][...]).astype(F32) for n in (2, 3)]
        buf[:, lead - RATE : lead, :] = jnp.where(west, near, far)
        buf[:, lead + 4 * breadth : lead + 4 * breadth + RATE, :] = jnp.where(west, far, near)
        for t in range(4):
            for c in (0, 2):
                first = lead + t * breadth + (c - 1) * RATE
                win = buf[:, first : first + breadth, :]
                o_ref[c, here ^ t] = win.reshape(step * breadth, filters).astype(BF)

    arrays = tuple(mine) + tuple(pair)
    return pl.pallas_call(
        body,
        grid_spec=pltpu.PrefetchScalarGridSpec(
            num_scalar_prefetch=1,
            grid=(rows // step,),
            in_specs=[
                pl.BlockSpec((step, x.shape[1], filters), lambda i, place: (i, 0, 0)) for x in arrays
            ],
            out_specs=pl.BlockSpec((3, 4, step * breadth, filters), lambda i, place: (0, 0, i, 0)),
            scratch_shapes=[pltpu.VMEM((step, wide, filters), F32)],
        ),
        out_shape=jax.ShapeDtypeStruct((3, 4, rows * breadth, filters), BF),
        compiler_params=pltpu.CompilerParams(vmem_limit_bytes=48 * 1024 * 1024),
    )(place.reshape(1).astype(jnp.int32), *arrays)


def grad_kernel(d_all, group_in, lats, lons, step_rows):
    filters = d_all.shape[3]
    width, cells = group_in[0].shape
    quarter = width // lats
    half_f = filters // lons // 2

    def body(d_ref, *refs):
        x_refs, o_ref = refs[:4], refs[4]
        for r in range(3):
            at = (2 - r) * step_rows
            acc = None
            for k in range(4):
                part = jnp.dot(x_refs[k][...], d_ref[0, k, at : at + cells, :], preferred_element_type=F32)
                acc = part if acc is None else acc + part
            out = acc.T
            for pair in range(lats // 2):
                both = out[:, pair * 2 * quarter : (pair + 1) * 2 * quarter]
                both = both.reshape(lons, 2, half_f, 2 * quarter)
                low, high = both[:, 0], both[:, 1]
                even = jnp.concatenate([low[..., :quarter], high[..., :quarter]], 2)
                odd = jnp.concatenate([low[..., quarter:], high[..., quarter:]], 2)
                o_ref[2 * pair, :, r, 0] = even.astype(BF)
                o_ref[2 * pair + 1, :, r, 0] = odd.astype(BF)

    return pl.pallas_call(
        body,
        grid=(3,),
        in_specs=[
            pl.BlockSpec((1,) + d_all.shape[1:], lambda c: (2 - c, 0, 0, 0)),
        ]
        + [pl.BlockSpec((width, cells), lambda c: (0, 0))] * 4,
        out_specs=pl.BlockSpec((lats, lons, 3, 1, half_f, 2 * quarter), lambda c: (0, 0, 0, c, 0, 0)),
        out_shape=jax.ShapeDtypeStruct((lats, lons, 3, 3, half_f, 2 * quarter), BF),
        compiler_params=pltpu.CompilerParams(vmem_limit_bytes=56 * 1024 * 1024),
    )(d_all, *group_in)


def grad_input(dcols, weight, cells, step_rows):
    channels, filters = weight.shape[1:]
    block = 512

    def body(d_ref, w_ref, o_ref):
        acc = None
        for r in range(3):
            for c in range(3):
                win = d_ref[2 - c, (2 - r) * step_rows : (2 - r) * step_rows + cells, :]
                part = lax.dot_general(
                    win, w_ref[r * 3 + c], (((1,), (1,)), ((), ())), preferred_element_type=F32
                )
                acc = part if acc is None else acc + part
        o_ref[...] = acc.astype(BF)

    return pl.pallas_call(
        body,
        grid=(channels // block,),
        in_specs=[
            pl.BlockSpec(dcols.shape, lambda n: (0, 0, 0)),
            pl.BlockSpec((9, block, filters), lambda n: (0, n, 0)),
        ],
        out_specs=pl.BlockSpec((cells, block), lambda n: (0, n)),
        out_shape=jax.ShapeDtypeStruct((cells, channels), BF),
        compiler_params=pltpu.CompilerParams(vmem_limit_bytes=48 * 1024 * 1024),
    )(dcols, weight)


def head(preact, labels, head_weight):
    hidden = jnp.maximum(preact, 0.0).astype(BF).astype(F32)
    logits = jnp.dot(hidden, head_weight.T, precision=lax.Precision.HIGHEST)
    classes = head_weight.shape[0]
    one_hot = (labels[:, None] == jnp.arange(classes, dtype=jnp.int32)[None, :]).astype(F32)
    exponent = jnp.exp(logits)
    partition = jnp.sum(exponent, 1, keepdims=True)
    grad_logits = exponent / partition - one_hot
    d_hidden = jnp.dot(grad_logits, head_weight, precision=lax.Precision.HIGHEST)
    d_preact = jnp.where(preact > 0, d_hidden, 0.0)
    return hidden, logits, one_hot, partition, grad_logits, d_preact


def shards(features, atrous_weight, norm_gain, norm_bias, head_weight, labels):
    height, breadth, channels = features.shape
    filters = atrous_weight.shape[3]
    classes = head_weight.shape[0]
    lats, lons = lax.axis_size("lat"), lax.axis_size("lon")
    lat = lax.axis_index("lat")
    place = lax.axis_index("lon") % 4
    cells = height * breadth
    total_cells = cells * lats * lons
    step_rows = RATE * breadth
    weight = atrous_weight.reshape(9, channels, filters)
    flat = features.reshape(cells, channels)

    rest = breadth - RATE
    outer = outer_rows(flat, weight, step_rows).reshape(2, 3, RATE, breadth, filters)
    outer, late_weight = lax.optimization_barrier((outer, weight))
    outer_w = ring(outer[:, 0, :, RATE:], "lon", 1, True)
    outer_e = ring(outer[:, 2, :, :rest], "lon", -1, True)
    sides = inner_rows(flat, late_weight, step_rows, (0, 2)).reshape(2, height, breadth, filters)
    inner_w = ring(sides[0, :, RATE:], "lon", 1, True)
    inner_e = ring(sides[1, :, :rest], "lon", -1, True)
    strips = outer[:, 1] + jnp.concatenate(
        [outer[:, 2, :, rest:] + outer_w, outer[:, 0, :, :RATE] + outer_e], 2
    )
    from_s = ring(strips[0], "lat", -1, False)
    from_n = ring(strips[1], "lat", 1, False)
    quarter = channels // (4 * lats)
    quarters = split_quarters(flat, place, quarter)
    inner_w, inner_e, quarters = lax.optimization_barrier((inner_w, inner_e, quarters))
    group_in = [quarters[0]] + [swap(quarters[k], k) for k in range(1, 4)]

    centre = inner_rows(flat, late_weight, step_rows, (1,)).reshape(height, breadth, filters)
    centre = centre + jnp.concatenate([sides[1, :, rest:] + inner_w, sides[0, :, :RATE] + inner_e], 1)

    zero = jnp.zeros((height - RATE, breadth, filters), F32)
    summed = (
        centre + jnp.concatenate([from_n, zero], 0) + jnp.concatenate([zero, from_s], 0)
    ).reshape(cells, filters)

    moments = total(jnp.stack([jnp.sum(summed, 0), jnp.sum(summed * summed, 0)]).reshape(-1, 128))
    moments, group_in[2] = lax.optimization_barrier((moments, group_in[2]))
    moments = moments.reshape(2, filters)
    average = moments[0] / total_cells
    variance = moments[1] / total_cells - average * average
    inverse = lax.rsqrt(variance + epsilon)
    normed = (summed - average) * inverse
    preact = norm_gain * normed + norm_bias

    pre_low = preact.astype(BF).reshape(height, breadth, filters)
    lab_low = labels.T.astype(BF)

    def with_labels(rows):
        lab = jnp.pad(lab_low[:, rows], ((0, 0), (0, filters - RATE)))
        return jnp.concatenate([pre_low[rows], lab[None]], 0)

    pre_n = ring(with_labels(slice(height - RATE, height)), "lat", 1, False)
    pre_s = ring(with_labels(slice(0, RATE)), "lat", -1, False)

    hidden, logits, one_hot, partition, grad_logits, d_preact = head(preact, labels.reshape(-1), head_weight)
    loss_terms = jnp.sum(jnp.log(partition)[:, 0] - jnp.sum(logits * one_hot, 1))
    head_term = jnp.dot(grad_logits.T, hidden, precision=lax.Precision.HIGHEST)
    payload = jnp.concatenate(
        [
            jnp.sum(d_preact, 0)[None],
            jnp.sum(d_preact * normed, 0)[None],
            head_term,
            jnp.broadcast_to(loss_terms, (1, filters)),
        ],
        0,
    )
    totals = total(payload.reshape(-1, 4, 128))
    totals, group_in[3] = lax.optimization_barrier((totals, group_in[3]))
    totals = totals.reshape(classes + 3, filters) / total_cells
    grad_bias, grad_gain, grad_head = totals[0], totals[1], totals[2 : 2 + classes]
    mean_loss = totals[2 + classes, 0]

    scale = norm_gain * inverse
    slope = inverse * grad_gain
    shift = slope * norm_bias - scale * grad_bias
    d_mid = (scale * (d_preact - grad_bias - normed * grad_gain)).astype(BF)
    wide = jnp.concatenate([pre_n[:RATE], pre_s[:RATE]], 0).astype(F32).reshape(2 * step_rows, filters)
    lab = jnp.concatenate([pre_n[RATE, :, :RATE], pre_s[RATE, :, :RATE]], 1).T.astype(jnp.int32)
    d_pre = head(wide, lab.reshape(2 * step_rows), head_weight)[-1]
    north = jnp.arange(2 * step_rows)[:, None] < step_rows
    exists = jnp.where(north, lat > 0, lat < lats - 1)
    d_halo = jnp.where(exists, scale * d_pre - slope * wide + shift, 0.0).astype(BF)
    d_col = jnp.concatenate([d_halo[:step_rows], d_mid, d_halo[step_rows:]], 0)
    d_col = d_col.reshape(height + 2 * RATE, breadth, filters)
    strip = jnp.where(place == 0, d_col[:, :RATE], d_col[:, breadth - RATE :])
    mine = (d_col, swap(d_col, 2), to_groups(strip, 1), to_groups(strip, 4))
    pair = [swap(x, 1) for x in mine]
    d_all = group_windows(place, mine, pair, breadth)

    blocks = grad_kernel(d_all, group_in, lats, lons, step_rows)
    blocks = blocks.reshape(lats * lons, -1, 2 * quarter)
    got = lax.all_to_all(blocks, ("lat", "lon"), 0, 0)
    own_f = filters // lons
    got = got.reshape(lats, lons // 4, 4, -1, 2 * quarter)
    weight_block = jnp.sum(got.astype(F32), (0, 1)) / total_cells
    weight_block = weight_block.reshape(4, 9, own_f // 2, 2, quarter)
    grad_weight = jnp.transpose(weight_block, (0, 4, 1, 3, 2)).reshape(4 * quarter, 3, 3, own_f)

    grad_features = grad_input(d_all[:, 0], weight, cells, step_rows).reshape(height, breadth, channels)
    return (mean_loss, grad_features, grad_weight, grad_gain, grad_bias, grad_head)


def solution(mesh):
    return jax.shard_map(
        shards,
        mesh=mesh,
        in_specs=(P("lat", "lon", None), P(), P(), P(), P(), P("lat", "lon")),
        out_specs=(P(), P("lat", "lon", None), P("lat", None, None, "lon"), P(), P(), P()),
        check_vma=False,
    )
```

```python
import math

import jax
import jax.numpy as jnp
from jax import lax
from jax.experimental import pallas as pl
from jax.experimental.pallas import tpu as pltpu
from jax.sharding import PartitionSpec as P

RATE = 12
epsilon = 1e-05
BF = jnp.bfloat16
F32 = jnp.float32


def ring(x, axis, step, periodic):
    count = lax.axis_size(axis)
    pairs = [(i, (i + step) % count) for i in range(count)]
    if not periodic:
        pairs = [(i, i + step) for i in range(count) if 0 <= i + step < count]
    return lax.ppermute(x, axis, pairs)


def swap(x, mask):
    count = lax.axis_size("lon")
    return lax.ppermute(x, "lon", [(i, i ^ mask) for i in range(count)])


def to_groups(x, gap):
    count = lax.axis_size("lon")
    pairs = []
    for first in range(0, count, 4):
        pairs.append((first + 3, (first + 3 + gap) % count))
        pairs.append((first, (first - gap) % count))
    return lax.ppermute(x, "lon", pairs)


def cost(flops, *arrays):
    size = sum(math.prod(x.shape) * x.dtype.itemsize for x in arrays)
    return pl.CostEstimate(flops=flops, transcendentals=0, bytes_accessed=size)


def total(x):
    count = lax.axis_size("lat") * lax.axis_size("lon")
    groups = [list(range(core, count, 2)) for core in range(2)]
    x = x + swap(x, 1)
    spread = jnp.broadcast_to(x[None], (count // 2,) + x.shape)
    return jnp.sum(lax.all_to_all(spread, ("lat", "lon"), 0, 0, axis_index_groups=groups), 0)


def outer_rows(flat, weight, edge):
    cells, channels = flat.shape
    filters = weight.shape[2]

    def body(x_ref, w_ref, o_ref):
        at = pl.ds(pl.multiple_of(pl.program_id(0) * (cells - edge), 16), edge)
        o_ref[0, 0] = jnp.dot(x_ref[at, :], w_ref[0], preferred_element_type=F32)

    return pl.pallas_call(
        body,
        grid=(2, 3),
        in_specs=[
            pl.BlockSpec((cells, channels), lambda e, c: (0, 0)),
            pl.BlockSpec((1, channels, filters), lambda e, c: ((1 - e) * 6 + c, 0, 0)),
        ],
        out_specs=pl.BlockSpec((1, 1, edge, filters), lambda e, c: (e, c, 0, 0)),
        out_shape=jax.ShapeDtypeStruct((2, 3, edge, filters), F32),
        cost_estimate=cost(12 * edge * channels * filters, flat, weight),
        compiler_params=pltpu.CompilerParams(vmem_limit_bytes=48 * 1024 * 1024),
    )(flat, weight)


def inner_rows(flat, weight, edge, cols):
    cells, channels = flat.shape
    filters = weight.shape[2]
    first, stride = cols[0], (cols[1] - cols[0]) if len(cols) > 1 else 1

    def body(x_ref, w_ref, o_ref):
        k = pl.program_id(1)

        @pl.when(k == 0)
        def _():
            o_ref[0] = jnp.dot(x_ref[...], w_ref[0], preferred_element_type=F32)

        @pl.when(k == 1)
        def _():
            o_ref[0, edge:, :] += jnp.dot(x_ref[: cells - edge, :], w_ref[0], preferred_element_type=F32)

        @pl.when(k == 2)
        def _():
            o_ref[0, : cells - edge, :] += jnp.dot(x_ref[edge:, :], w_ref[0], preferred_element_type=F32)

    def tap(c, k):
        return ((k * k * 3 - k * 5 + 2) // 2 * 3 + first + c * stride, 0, 0)

    return pl.pallas_call(
        body,
        grid=(len(cols), 3),
        in_specs=[
            pl.BlockSpec((cells, channels), lambda c, k: (0, 0)),
            pl.BlockSpec((1, channels, filters), tap),
        ],
        out_specs=pl.BlockSpec((1, cells, filters), lambda c, k: (c, 0, 0)),
        out_shape=jax.ShapeDtypeStruct((len(cols), cells, filters), F32),
        cost_estimate=cost(6 * len(cols) * cells * channels * filters, flat),
        compiler_params=pltpu.CompilerParams(vmem_limit_bytes=48 * 1024 * 1024),
    )(flat, weight)


def split_quarters(flat, where, quarter):
    cells, channels = flat.shape
    blocks = channels // (4 * quarter)

    def body(where_ref, x_ref, *o_refs):
        parts = []
        for t in range(4):
            left = x_ref[:, t * quarter : (t + 1) * quarter]
            right = x_ref[:, (4 + t) * quarter : (5 + t) * quarter]
            parts.append(jnp.concatenate([left, right], 1).T)
        for here in range(4):

            @pl.when(where_ref[0] == here)
            def _():
                for t in range(4):
                    o_refs[here ^ t][...] = parts[t]

    return pl.pallas_call(
        body,
        grid_spec=pltpu.PrefetchScalarGridSpec(
            num_scalar_prefetch=1,
            grid=(blocks // 2,),
            in_specs=[pl.BlockSpec((cells, 8 * quarter), lambda i, w: (0, i))],
            out_specs=[pl.BlockSpec((2 * quarter, cells), lambda i, w: (i, 0))] * 4,
        ),
        out_shape=[jax.ShapeDtypeStruct((blocks * quarter, cells), BF)] * 4,
        cost_estimate=cost(0, flat, flat),
        compiler_params=pltpu.CompilerParams(vmem_limit_bytes=48 * 1024 * 1024),
    )(where.reshape(1).astype(jnp.int32), flat)


def group_windows(place, mine, pair, breadth):
    rows, _, filters = mine[0].shape
    step, lead = 8, 16
    wide = lead + 4 * breadth + lead

    def body(place_ref, *refs):
        parts, o_ref, buf = refs[:8], refs[8], refs[9]
        here = place_ref[0]
        order = (0, 4, 1, 5)
        for k in range(4):
            first = pl.multiple_of(lead + breadth * (here ^ k), 8)
            d = parts[order[k]][...]
            o_ref[1, k] = d.reshape(step * breadth, filters)
            buf[:, pl.ds(first, breadth), :] = d.astype(F32)
        ends = (here == 0) | (here == 3)
        west = here < 2
        near, far = [jnp.where(ends, parts[n][...], parts[4 + n][...]).astype(F32) for n in (2, 3)]
        buf[:, lead - RATE : lead, :] = jnp.where(west, near, far)
        buf[:, lead + 4 * breadth : lead + 4 * breadth + RATE, :] = jnp.where(west, far, near)
        for t in range(4):
            for c in (0, 2):
                first = lead + t * breadth + (c - 1) * RATE
                win = buf[:, first : first + breadth, :]
                o_ref[c, here ^ t] = win.reshape(step * breadth, filters).astype(BF)

    arrays = tuple(mine) + tuple(pair)
    return pl.pallas_call(
        body,
        grid_spec=pltpu.PrefetchScalarGridSpec(
            num_scalar_prefetch=1,
            grid=(rows // step,),
            in_specs=[
                pl.BlockSpec((step, x.shape[1], filters), lambda i, place: (i, 0, 0)) for x in arrays
            ],
            out_specs=pl.BlockSpec((3, 4, step * breadth, filters), lambda i, place: (0, 0, i, 0)),
            scratch_shapes=[pltpu.VMEM((step, wide, filters), F32)],
        ),
        out_shape=jax.ShapeDtypeStruct((3, 4, rows * breadth, filters), BF),
        cost_estimate=cost(0, *arrays, *arrays),
        compiler_params=pltpu.CompilerParams(vmem_limit_bytes=48 * 1024 * 1024),
    )(place.reshape(1).astype(jnp.int32), *arrays)


def grad_kernel(d_all, group_in, lats, lons, step_rows):
    filters = d_all.shape[3]
    width, cells = group_in[0].shape
    quarter = width // lats
    half_f = filters // lons // 2

    def body(d_ref, *refs):
        x_refs, o_ref = refs[:4], refs[4]
        for r in range(3):
            at = (2 - r) * step_rows
            acc = None
            for k in range(4):
                part = jnp.dot(x_refs[k][...], d_ref[0, k, at : at + cells, :], preferred_element_type=F32)
                acc = part if acc is None else acc + part
            out = acc.T
            for pair in range(lats // 2):
                both = out[:, pair * 2 * quarter : (pair + 1) * 2 * quarter]
                both = both.reshape(lons, 2, half_f, 2 * quarter)
                low, high = both[:, 0], both[:, 1]
                even = jnp.concatenate([low[..., :quarter], high[..., :quarter]], 2)
                odd = jnp.concatenate([low[..., quarter:], high[..., quarter:]], 2)
                o_ref[2 * pair, :, r, 0] = even.astype(BF)
                o_ref[2 * pair + 1, :, r, 0] = odd.astype(BF)

    return pl.pallas_call(
        body,
        grid=(3,),
        in_specs=[
            pl.BlockSpec((1,) + d_all.shape[1:], lambda c: (2 - c, 0, 0, 0)),
        ]
        + [pl.BlockSpec((width, cells), lambda c: (0, 0))] * 4,
        out_specs=pl.BlockSpec((lats, lons, 3, 1, half_f, 2 * quarter), lambda c: (0, 0, 0, c, 0, 0)),
        out_shape=jax.ShapeDtypeStruct((lats, lons, 3, 3, half_f, 2 * quarter), BF),
        cost_estimate=cost(72 * cells * width * filters, d_all, *group_in),
        compiler_params=pltpu.CompilerParams(vmem_limit_bytes=56 * 1024 * 1024),
    )(d_all, *group_in)


def grad_input(dcols, weight, cells, step_rows):
    channels, filters = weight.shape[1:]
    block = 512

    def body(d_ref, w_ref, o_ref):
        acc = None
        for r in range(3):
            for c in range(3):
                win = d_ref[2 - c, (2 - r) * step_rows : (2 - r) * step_rows + cells, :]
                part = lax.dot_general(
                    win, w_ref[r * 3 + c], (((1,), (1,)), ((), ())), preferred_element_type=F32
                )
                acc = part if acc is None else acc + part
        o_ref[...] = acc.astype(BF)

    return pl.pallas_call(
        body,
        grid=(channels // block,),
        in_specs=[
            pl.BlockSpec(dcols.shape, lambda n: (0, 0, 0)),
            pl.BlockSpec((9, block, filters), lambda n: (0, n, 0)),
        ],
        out_specs=pl.BlockSpec((cells, block), lambda n: (0, n)),
        out_shape=jax.ShapeDtypeStruct((cells, channels), BF),
        cost_estimate=cost(18 * cells * channels * filters, weight),
        compiler_params=pltpu.CompilerParams(vmem_limit_bytes=48 * 1024 * 1024),
    )(dcols, weight)


def head(preact, labels, head_weight):
    hidden = jnp.maximum(preact, 0.0).astype(BF).astype(F32)
    logits = jnp.dot(hidden, head_weight.T, precision=lax.Precision.HIGHEST)
    classes = head_weight.shape[0]
    one_hot = (labels[:, None] == jnp.arange(classes, dtype=jnp.int32)[None, :]).astype(F32)
    exponent = jnp.exp(logits)
    partition = jnp.sum(exponent, 1, keepdims=True)
    grad_logits = exponent / partition - one_hot
    d_hidden = jnp.dot(grad_logits, head_weight, precision=lax.Precision.HIGHEST)
    d_preact = jnp.where(preact > 0, d_hidden, 0.0)
    return hidden, logits, one_hot, partition, grad_logits, d_preact


def shards(features, atrous_weight, norm_gain, norm_bias, head_weight, labels):
    height, breadth, channels = features.shape
    filters = atrous_weight.shape[3]
    classes = head_weight.shape[0]
    lats, lons = lax.axis_size("lat"), lax.axis_size("lon")
    lat = lax.axis_index("lat")
    place = lax.axis_index("lon") % 4
    cells = height * breadth
    total_cells = cells * lats * lons
    step_rows = RATE * breadth
    weight = atrous_weight.reshape(9, channels, filters)
    flat = features.reshape(cells, channels)

    rest = breadth - RATE
    outer = outer_rows(flat, weight, step_rows).reshape(2, 3, RATE, breadth, filters)
    outer, late_weight = lax.optimization_barrier((outer, weight))
    outer_w = ring(outer[:, 0, :, RATE:], "lon", 1, True)
    outer_e = ring(outer[:, 2, :, :rest], "lon", -1, True)
    sides = inner_rows(flat, late_weight, step_rows, (0, 2)).reshape(2, height, breadth, filters)
    inner_w = ring(sides[0, :, RATE:], "lon", 1, True)
    inner_e = ring(sides[1, :, :rest], "lon", -1, True)
    strips = outer[:, 1] + jnp.concatenate(
        [outer[:, 2, :, rest:] + outer_w, outer[:, 0, :, :RATE] + outer_e], 2
    )
    from_s = ring(strips[0], "lat", -1, False)
    from_n = ring(strips[1], "lat", 1, False)
    quarter = channels // (4 * lats)
    quarters = split_quarters(flat, place, quarter)
    inner_w, inner_e, quarters = lax.optimization_barrier((inner_w, inner_e, quarters))
    group_in = [quarters[0]] + [swap(quarters[k], k) for k in range(1, 4)]

    centre = inner_rows(flat, late_weight, step_rows, (1,)).reshape(height, breadth, filters)
    centre = centre + jnp.concatenate([sides[1, :, rest:] + inner_w, sides[0, :, :RATE] + inner_e], 1)

    zero = jnp.zeros((height - RATE, breadth, filters), F32)
    summed = (
        centre + jnp.concatenate([from_n, zero], 0) + jnp.concatenate([zero, from_s], 0)
    ).reshape(cells, filters)

    moments = total(jnp.stack([jnp.sum(summed, 0), jnp.sum(summed * summed, 0)]).reshape(-1, 128))
    moments, group_in[2] = lax.optimization_barrier((moments, group_in[2]))
    moments = moments.reshape(2, filters)
    average = moments[0] / total_cells
    variance = moments[1] / total_cells - average * average
    inverse = lax.rsqrt(variance + epsilon)
    normed = (summed - average) * inverse
    preact = norm_gain * normed + norm_bias

    pre_low = preact.astype(BF).reshape(height, breadth, filters)
    lab_low = labels.T.astype(BF)

    def with_labels(rows):
        lab = jnp.pad(lab_low[:, rows], ((0, 0), (0, filters - RATE)))
        return jnp.concatenate([pre_low[rows], lab[None]], 0)

    pre_n = ring(with_labels(slice(height - RATE, height)), "lat", 1, False)
    pre_s = ring(with_labels(slice(0, RATE)), "lat", -1, False)

    hidden, logits, one_hot, partition, grad_logits, d_preact = head(preact, labels.reshape(-1), head_weight)
    loss_terms = jnp.sum(jnp.log(partition)[:, 0] - jnp.sum(logits * one_hot, 1))
    head_term = jnp.dot(grad_logits.T, hidden, precision=lax.Precision.HIGHEST)
    payload = jnp.concatenate(
        [
            jnp.sum(d_preact, 0)[None],
            jnp.sum(d_preact * normed, 0)[None],
            head_term,
            jnp.broadcast_to(loss_terms, (1, filters)),
        ],
        0,
    )
    totals = total(payload.reshape(-1, 4, 128))
    totals, group_in[3] = lax.optimization_barrier((totals, group_in[3]))
    totals = totals.reshape(classes + 3, filters) / total_cells
    grad_bias, grad_gain, grad_head = totals[0], totals[1], totals[2 : 2 + classes]
    mean_loss = totals[2 + classes, 0]

    scale = norm_gain * inverse
    slope = inverse * grad_gain
    shift = slope * norm_bias - scale * grad_bias
    d_mid = (scale * (d_preact - grad_bias - normed * grad_gain)).astype(BF)
    wide = jnp.concatenate([pre_n[:RATE], pre_s[:RATE]], 0).astype(F32).reshape(2 * step_rows, filters)
    lab = jnp.concatenate([pre_n[RATE, :, :RATE], pre_s[RATE, :, :RATE]], 1).T.astype(jnp.int32)
    d_pre = head(wide, lab.reshape(2 * step_rows), head_weight)[-1]
    north = jnp.arange(2 * step_rows)[:, None] < step_rows
    exists = jnp.where(north, lat > 0, lat < lats - 1)
    d_halo = jnp.where(exists, scale * d_pre - slope * wide + shift, 0.0).astype(BF)
    d_col = jnp.concatenate([d_halo[:step_rows], d_mid, d_halo[step_rows:]], 0)
    d_col = d_col.reshape(height + 2 * RATE, breadth, filters)
    strip = jnp.where(place == 0, d_col[:, :RATE], d_col[:, breadth - RATE :])
    mine = (d_col, swap(d_col, 2), to_groups(strip, 1), to_groups(strip, 4))
    pair = [swap(x, 1) for x in mine]
    d_all = group_windows(place, mine, pair, breadth)

    blocks = grad_kernel(d_all, group_in, lats, lons, step_rows)
    blocks = blocks.reshape(lats * lons, -1, 2 * quarter)
    got = lax.all_to_all(blocks, ("lat", "lon"), 0, 0)
    own_f = filters // lons
    got = got.reshape(lats, lons // 4, 4, -1, 2 * quarter)
    weight_block = jnp.sum(got.astype(F32), (0, 1)) / total_cells
    weight_block = weight_block.reshape(4, 9, own_f // 2, 2, quarter)
    grad_weight = jnp.transpose(weight_block, (0, 4, 1, 3, 2)).reshape(4 * quarter, 3, 3, own_f)

    grad_features = grad_input(d_all[:, 0], weight, cells, step_rows).reshape(height, breadth, channels)
    return (mean_loss, grad_features, grad_weight, grad_gain, grad_bias, grad_head)


def solution(mesh):
    return jax.shard_map(
        shards,
        mesh=mesh,
        in_specs=(P("lat", "lon", None), P(), P(), P(), P(), P("lat", "lon")),
        out_specs=(P(), P("lat", "lon", None), P("lat", None, None, "lon"), P(), P(), P()),
        check_vma=False,
    )
```

```python
import math

import jax
import jax.numpy as jnp
from jax import lax
from jax.experimental import pallas as pl
from jax.experimental.pallas import tpu as pltpu
from jax.sharding import PartitionSpec as P

RATE = 12
epsilon = 1e-05
BF = jnp.bfloat16
F32 = jnp.float32


def ring(x, axis, step, periodic):
    count = lax.axis_size(axis)
    pairs = [(i, (i + step) % count) for i in range(count)]
    if not periodic:
        pairs = [(i, i + step) for i in range(count) if 0 <= i + step < count]
    return lax.ppermute(x, axis, pairs)


def swap(x, mask):
    count = lax.axis_size("lon")
    return lax.ppermute(x, "lon", [(i, i ^ mask) for i in range(count)])


def to_groups(x, gap):
    count = lax.axis_size("lon")
    pairs = []
    for first in range(0, count, 4):
        pairs.append((first + 3, (first + 3 + gap) % count))
        pairs.append((first, (first - gap) % count))
    return lax.ppermute(x, "lon", pairs)


def cost(flops, *arrays):
    size = sum(math.prod(x.shape) * x.dtype.itemsize for x in arrays)
    return pl.CostEstimate(flops=flops, transcendentals=0, bytes_accessed=size)


def total(x):
    count = lax.axis_size("lat") * lax.axis_size("lon")
    groups = [list(range(core, count, 2)) for core in range(2)]
    x = x + swap(x, 1)
    spread = jnp.broadcast_to(x[None], (count // 2,) + x.shape)
    return jnp.sum(lax.all_to_all(spread, ("lat", "lon"), 0, 0, axis_index_groups=groups), 0)


def outer_rows(flat, weight, edge):
    cells, channels = flat.shape
    filters = weight.shape[2]

    def body(x_ref, w_ref, o_ref):
        at = pl.ds(pl.multiple_of(pl.program_id(0) * (cells - edge), 16), edge)
        o_ref[0, 0] = jnp.dot(x_ref[at, :], w_ref[0], preferred_element_type=F32)

    return pl.pallas_call(
        body,
        grid=(2, 3),
        in_specs=[
            pl.BlockSpec((cells, channels), lambda e, c: (0, 0)),
            pl.BlockSpec((1, channels, filters), lambda e, c: ((1 - e) * 6 + c, 0, 0)),
        ],
        out_specs=pl.BlockSpec((1, 1, edge, filters), lambda e, c: (e, c, 0, 0)),
        out_shape=jax.ShapeDtypeStruct((2, 3, edge, filters), F32),
        cost_estimate=cost(12 * edge * channels * filters, flat, weight),
        compiler_params=pltpu.CompilerParams(vmem_limit_bytes=20 * 1024 * 1024),
    )(flat, weight)


def inner_rows(flat, weight, edge, cols):
    cells, channels = flat.shape
    filters = weight.shape[2]
    first, stride = cols[0], (cols[1] - cols[0]) if len(cols) > 1 else 1

    def body(x_ref, w_ref, o_ref):
        k = pl.program_id(1)

        @pl.when(k == 0)
        def _():
            o_ref[0] = jnp.dot(x_ref[...], w_ref[0], preferred_element_type=F32)

        @pl.when(k == 1)
        def _():
            o_ref[0, edge:, :] += jnp.dot(x_ref[: cells - edge, :], w_ref[0], preferred_element_type=F32)

        @pl.when(k == 2)
        def _():
            o_ref[0, : cells - edge, :] += jnp.dot(x_ref[edge:, :], w_ref[0], preferred_element_type=F32)

    def tap(c, k):
        return ((k * k * 3 - k * 5 + 2) // 2 * 3 + first + c * stride, 0, 0)

    return pl.pallas_call(
        body,
        grid=(len(cols), 3),
        in_specs=[
            pl.BlockSpec((cells, channels), lambda c, k: (0, 0)),
            pl.BlockSpec((1, channels, filters), tap),
        ],
        out_specs=pl.BlockSpec((1, cells, filters), lambda c, k: (c, 0, 0)),
        out_shape=jax.ShapeDtypeStruct((len(cols), cells, filters), F32),
        cost_estimate=cost(6 * len(cols) * cells * channels * filters, flat),
        compiler_params=pltpu.CompilerParams(vmem_limit_bytes=24 * 1024 * 1024),
    )(flat, weight)


def split_quarters(flat, where, quarter):
    cells, channels = flat.shape
    blocks = channels // (4 * quarter)

    def body(where_ref, x_ref, *o_refs):
        parts = []
        for t in range(4):
            left = x_ref[:, t * quarter : (t + 1) * quarter]
            right = x_ref[:, (4 + t) * quarter : (5 + t) * quarter]
            parts.append(jnp.concatenate([left, right], 1).T)
        for here in range(4):

            @pl.when(where_ref[0] == here)
            def _():
                for t in range(4):
                    o_refs[here ^ t][...] = parts[t]

    return pl.pallas_call(
        body,
        grid_spec=pltpu.PrefetchScalarGridSpec(
            num_scalar_prefetch=1,
            grid=(blocks // 2,),
            in_specs=[pl.BlockSpec((cells, 8 * quarter), lambda i, w: (0, i))],
            out_specs=[pl.BlockSpec((2 * quarter, cells), lambda i, w: (i, 0))] * 4,
        ),
        out_shape=[jax.ShapeDtypeStruct((blocks * quarter, cells), BF)] * 4,
        cost_estimate=cost(0, flat, flat),
        compiler_params=pltpu.CompilerParams(vmem_limit_bytes=20 * 1024 * 1024),
    )(where.reshape(1).astype(jnp.int32), flat)


def group_windows(place, mine, pair, breadth):
    rows, _, filters = mine[0].shape
    step, lead = 8, 16
    wide = lead + 4 * breadth + lead

    def body(place_ref, *refs):
        parts, o_ref, buf = refs[:8], refs[8], refs[9]
        here = place_ref[0]
        order = (0, 4, 1, 5)
        for k in range(4):
            first = pl.multiple_of(lead + breadth * (here ^ k), 8)
            d = parts[order[k]][...]
            o_ref[1, k] = d.reshape(step * breadth, filters)
            buf[:, pl.ds(first, breadth), :] = d.astype(F32)
        ends = (here == 0) | (here == 3)
        west = here < 2
        near, far = [jnp.where(ends, parts[n][...], parts[4 + n][...]).astype(F32) for n in (2, 3)]
        buf[:, lead - RATE : lead, :] = jnp.where(west, near, far)
        buf[:, lead + 4 * breadth : lead + 4 * breadth + RATE, :] = jnp.where(west, far, near)
        for t in range(4):
            for c in (0, 2):
                first = lead + t * breadth + (c - 1) * RATE
                win = buf[:, first : first + breadth, :]
                o_ref[c, here ^ t] = win.reshape(step * breadth, filters).astype(BF)

    arrays = tuple(mine) + tuple(pair)
    return pl.pallas_call(
        body,
        grid_spec=pltpu.PrefetchScalarGridSpec(
            num_scalar_prefetch=1,
            grid=(rows // step,),
            in_specs=[
                pl.BlockSpec((step, x.shape[1], filters), lambda i, place: (i, 0, 0)) for x in arrays
            ],
            out_specs=pl.BlockSpec((3, 4, step * breadth, filters), lambda i, place: (0, 0, i, 0)),
            scratch_shapes=[pltpu.VMEM((step, wide, filters), F32)],
        ),
        out_shape=jax.ShapeDtypeStruct((3, 4, rows * breadth, filters), BF),
        cost_estimate=cost(0, *arrays, *arrays),
        compiler_params=pltpu.CompilerParams(vmem_limit_bytes=16 * 1024 * 1024),
    )(place.reshape(1).astype(jnp.int32), *arrays)


def grad_kernel(d_all, group_in, lats, lons, step_rows):
    filters = d_all.shape[3]
    width, cells = group_in[0].shape
    quarter = width // lats
    half_f = filters // lons // 2

    def body(d_ref, *refs):
        x_refs, o_ref = refs[:4], refs[4]
        for r in range(3):
            at = (2 - r) * step_rows
            acc = None
            for k in range(4):
                part = jnp.dot(x_refs[k][...], d_ref[0, k, at : at + cells, :], preferred_element_type=F32)
                acc = part if acc is None else acc + part
            out = acc.T
            for pair in range(lats // 2):
                both = out[:, pair * 2 * quarter : (pair + 1) * 2 * quarter]
                both = both.reshape(lons, 2, half_f, 2 * quarter)
                low, high = both[:, 0], both[:, 1]
                even = jnp.concatenate([low[..., :quarter], high[..., :quarter]], 2)
                odd = jnp.concatenate([low[..., quarter:], high[..., quarter:]], 2)
                o_ref[2 * pair, :, r, 0] = even.astype(BF)
                o_ref[2 * pair + 1, :, r, 0] = odd.astype(BF)

    return pl.pallas_call(
        body,
        grid=(3,),
        in_specs=[
            pl.BlockSpec((1,) + d_all.shape[1:], lambda c: (2 - c, 0, 0, 0)),
        ]
        + [pl.BlockSpec((width, cells), lambda c: (0, 0))] * 4,
        out_specs=pl.BlockSpec((lats, lons, 3, 1, half_f, 2 * quarter), lambda c: (0, 0, 0, c, 0, 0)),
        out_shape=jax.ShapeDtypeStruct((lats, lons, 3, 3, half_f, 2 * quarter), BF),
        cost_estimate=cost(72 * cells * width * filters, d_all, *group_in),
        compiler_params=pltpu.CompilerParams(vmem_limit_bytes=32 * 1024 * 1024),
    )(d_all, *group_in)


def grad_input(dcols, weight, cells, step_rows):
    channels, filters = weight.shape[1:]
    block = 512

    def body(d_ref, w_ref, o_ref):
        acc = None
        for r in range(3):
            for c in range(3):
                win = d_ref[2 - c, (2 - r) * step_rows : (2 - r) * step_rows + cells, :]
                part = lax.dot_general(
                    win, w_ref[r * 3 + c], (((1,), (1,)), ((), ())), preferred_element_type=F32
                )
                acc = part if acc is None else acc + part
        o_ref[...] = acc.astype(BF)

    return pl.pallas_call(
        body,
        grid=(channels // block,),
        in_specs=[
            pl.BlockSpec(dcols.shape, lambda n: (0, 0, 0)),
            pl.BlockSpec((9, block, filters), lambda n: (0, n, 0)),
        ],
        out_specs=pl.BlockSpec((cells, block), lambda n: (0, n)),
        out_shape=jax.ShapeDtypeStruct((cells, channels), BF),
        cost_estimate=cost(18 * cells * channels * filters, weight),
        compiler_params=pltpu.CompilerParams(vmem_limit_bytes=32 * 1024 * 1024),
    )(dcols, weight)


def head(preact, labels, head_weight):
    hidden = jnp.maximum(preact, 0.0).astype(BF).astype(F32)
    logits = jnp.dot(hidden, head_weight.T, precision=lax.Precision.HIGHEST)
    classes = head_weight.shape[0]
    one_hot = (labels[:, None] == jnp.arange(classes, dtype=jnp.int32)[None, :]).astype(F32)
    exponent = jnp.exp(logits)
    partition = jnp.sum(exponent, 1, keepdims=True)
    grad_logits = exponent / partition - one_hot
    d_hidden = jnp.dot(grad_logits, head_weight, precision=lax.Precision.HIGHEST)
    d_preact = jnp.where(preact > 0, d_hidden, 0.0)
    return hidden, logits, one_hot, partition, grad_logits, d_preact


def shards(features, atrous_weight, norm_gain, norm_bias, head_weight, labels):
    height, breadth, channels = features.shape
    filters = atrous_weight.shape[3]
    classes = head_weight.shape[0]
    lats, lons = lax.axis_size("lat"), lax.axis_size("lon")
    lat = lax.axis_index("lat")
    place = lax.axis_index("lon") % 4
    cells = height * breadth
    total_cells = cells * lats * lons
    step_rows = RATE * breadth
    weight = atrous_weight.reshape(9, channels, filters)
    flat = features.reshape(cells, channels)

    rest = breadth - RATE
    outer = outer_rows(flat, weight, step_rows).reshape(2, 3, RATE, breadth, filters)
    outer, late_weight = lax.optimization_barrier((outer, weight))
    outer_w = ring(outer[:, 0, :, RATE:], "lon", 1, True)
    outer_e = ring(outer[:, 2, :, :rest], "lon", -1, True)
    sides = inner_rows(flat, late_weight, step_rows, (0, 2)).reshape(2, height, breadth, filters)
    inner_w = ring(sides[0, :, RATE:], "lon", 1, True)
    inner_e = ring(sides[1, :, :rest], "lon", -1, True)
    strips = outer[:, 1] + jnp.concatenate(
        [outer[:, 2, :, rest:] + outer_w, outer[:, 0, :, :RATE] + outer_e], 2
    )
    from_s = ring(strips[0], "lat", -1, False)
    from_n = ring(strips[1], "lat", 1, False)
    quarter = channels // (4 * lats)
    quarters = split_quarters(flat, place, quarter)
    inner_w, inner_e, quarters = lax.optimization_barrier((inner_w, inner_e, quarters))
    group_in = [quarters[0]] + [swap(quarters[k], k) for k in range(1, 4)]

    centre = inner_rows(flat, late_weight, step_rows, (1,)).reshape(height, breadth, filters)
    centre = centre + jnp.concatenate([sides[1, :, rest:] + inner_w, sides[0, :, :RATE] + inner_e], 1)

    zero = jnp.zeros((height - RATE, breadth, filters), F32)
    summed = (
        centre + jnp.concatenate([from_n, zero], 0) + jnp.concatenate([zero, from_s], 0)
    ).reshape(cells, filters)

    moments = total(jnp.stack([jnp.sum(summed, 0), jnp.sum(summed * summed, 0)]).reshape(-1, 128))
    moments, group_in[2] = lax.optimization_barrier((moments, group_in[2]))
    moments = moments.reshape(2, filters)
    average = moments[0] / total_cells
    variance = moments[1] / total_cells - average * average
    inverse = lax.rsqrt(variance + epsilon)
    normed = (summed - average) * inverse
    preact = norm_gain * normed + norm_bias

    pre_low = preact.astype(BF).reshape(height, breadth, filters)
    lab_low = labels.T.astype(BF)

    def with_labels(rows):
        lab = jnp.pad(lab_low[:, rows], ((0, 0), (0, filters - RATE)))
        return jnp.concatenate([pre_low[rows], lab[None]], 0)

    pre_n = ring(with_labels(slice(height - RATE, height)), "lat", 1, False)
    pre_s = ring(with_labels(slice(0, RATE)), "lat", -1, False)

    hidden, logits, one_hot, partition, grad_logits, d_preact = head(preact, labels.reshape(-1), head_weight)
    loss_terms = jnp.sum(jnp.log(partition)[:, 0] - jnp.sum(logits * one_hot, 1))
    head_term = jnp.dot(grad_logits.T, hidden, precision=lax.Precision.HIGHEST)
    payload = jnp.concatenate(
        [
            jnp.sum(d_preact, 0)[None],
            jnp.sum(d_preact * normed, 0)[None],
            head_term,
            jnp.broadcast_to(loss_terms, (1, filters)),
        ],
        0,
    )
    totals = total(payload.reshape(-1, 4, 128))
    totals, group_in[3] = lax.optimization_barrier((totals, group_in[3]))
    totals = totals.reshape(classes + 3, filters) / total_cells
    grad_bias, grad_gain, grad_head = totals[0], totals[1], totals[2 : 2 + classes]
    mean_loss = totals[2 + classes, 0]

    scale = norm_gain * inverse
    slope = inverse * grad_gain
    shift = slope * norm_bias - scale * grad_bias
    d_mid = (scale * (d_preact - grad_bias - normed * grad_gain)).astype(BF)
    wide = jnp.concatenate([pre_n[:RATE], pre_s[:RATE]], 0).astype(F32).reshape(2 * step_rows, filters)
    lab = jnp.concatenate([pre_n[RATE, :, :RATE], pre_s[RATE, :, :RATE]], 1).T.astype(jnp.int32)
    d_pre = head(wide, lab.reshape(2 * step_rows), head_weight)[-1]
    north = jnp.arange(2 * step_rows)[:, None] < step_rows
    exists = jnp.where(north, lat > 0, lat < lats - 1)
    d_halo = jnp.where(exists, scale * d_pre - slope * wide + shift, 0.0).astype(BF)
    d_col = jnp.concatenate([d_halo[:step_rows], d_mid, d_halo[step_rows:]], 0)
    d_col = d_col.reshape(height + 2 * RATE, breadth, filters)
    strip = jnp.where(place == 0, d_col[:, :RATE], d_col[:, breadth - RATE :])
    mine = (d_col, swap(d_col, 2), to_groups(strip, 1), to_groups(strip, 4))
    pair = [swap(x, 1) for x in mine]
    d_all = group_windows(place, mine, pair, breadth)

    blocks = grad_kernel(d_all, group_in, lats, lons, step_rows)
    blocks = blocks.reshape(lats * lons, -1, 2 * quarter)
    got = lax.all_to_all(blocks, ("lat", "lon"), 0, 0)
    own_f = filters // lons
    got = got.reshape(lats, lons // 4, 4, -1, 2 * quarter)
    weight_block = jnp.sum(got.astype(F32), (0, 1)) / total_cells
    weight_block = weight_block.reshape(4, 9, own_f // 2, 2, quarter)
    grad_weight = jnp.transpose(weight_block, (0, 4, 1, 3, 2)).reshape(4 * quarter, 3, 3, own_f)

    grad_features = grad_input(d_all[:, 0], weight, cells, step_rows).reshape(height, breadth, channels)
    return (mean_loss, grad_features, grad_weight, grad_gain, grad_bias, grad_head)


def solution(mesh):
    return jax.shard_map(
        shards,
        mesh=mesh,
        in_specs=(P("lat", "lon", None), P(), P(), P(), P(), P("lat", "lon")),
        out_specs=(P(), P("lat", "lon", None), P("lat", None, None, "lon"), P(), P(), P()),
        check_vma=False,
    )
```
